256 devices in a mesh: gx: 16 (over y, x_hi, core), gy: 16 (over x_lo, z).
Axes of the slice: x: 4 (x_hi: 2, x_lo: 2; x = x_hi * 2 + x_lo), y: 4, z: 8, core: 2. Of those that a mesh axis runs over, the one named last changes fastest.
Arguments:
- source: bfloat16 [64, 32, 128, 128], P(None, 'gx', 'gy'), may hold values from -6 to 6
- preact: bfloat16 [64, 32, 128, 128], P(None, 'gx', 'gy'), may hold values from -6 to 6
- cotangent: bfloat16 [64, 32, 128, 128], P(None, 'gx', 'gy'), may hold values from -6 to 6
- kernel: bfloat16 [27, 64, 64], replicated, may hold values from -0.15625 to 0.15625
Outputs:
- grad_source: bfloat16 [64, 32, 128, 128], P(None, 'gx', 'gy')
- grad_kernel: float32 [110592], P(('gx', 'gy'))
The draws below stay inside these ranges and needn't reach their ends.
All inputs are finite; a program needn't handle non-finite values.
Results may differ from the reference program's by a relative error of at most 0.007.
Values may be sent and summed in bfloat16 or wider, within the bound.
A program may use at most 64 MiB of HBM per device.

```python
import jax
import jax.numpy as jnp
from jax import lax

C = 64
NZ = 128
NX = 32
NY = 128


def block_scale(stream_key, extent, split, least, largest):
    def one(axis_at, parts):
        steps = jax.random.uniform(jax.random.fold_in(jax.random.fold_in(stream_key, 6), axis_at), (parts,), jnp.float32, least / len(split), largest / len(split))
        return jnp.repeat(jnp.exp(steps), extent[axis_at] // parts).reshape((-1,) + (1,) * (len(extent) - axis_at - 1))

    loudness = one(*split[0])
    for cut in split[1:]:
        loudness = loudness * one(*cut)
    return loudness


def centred(own_key, dims, deviation, reach, shards=(), kind=jnp.bfloat16):
    result = deviation * jax.random.normal(own_key, dims, jnp.float32)
    if shards:
        result = result * block_scale(own_key, dims, shards, -0.22, 0.18)
    return jnp.clip(result, -reach, reach).astype(kind)


def setup_inputs(seed: int = 0) -> dict:
    key_list = jax.random.split(jax.random.key(seed), 5)
    source = centred(key_list[0], (C, NX, NY, NZ), 1.0, 6.0, ((1, 16), (2, 16)))
    preact = centred(key_list[1], (C, NX, NY, NZ), 1.0, 6.0, ((1, 16), (2, 16)))
    cotangent = centred(key_list[2], (C, NX, NY, NZ), 1.0, 6.0, ((1, 16), (2, 16)))
    kernel = centred(key_list[3], (27, C, C), (27 * C) ** -0.5, 0.15625)
    return dict(source=source, preact=preact, cotangent=cotangent, kernel=kernel)


def reference(source, preact, cotangent, kernel):
    channels = source.shape[0]
    slope_grad = jnp.where(preact > 0, cotangent, jnp.zeros_like(cotangent))
    source_f = source.astype(jnp.float32)
    slope_f = slope_grad.astype(jnp.float32)
    kernel_f = kernel.astype(jnp.float32)
    slope_flat = slope_f.reshape(channels, -1)
    grad_source = jnp.zeros(slope_flat.shape, jnp.float32)
    pieces = []
    for a in range(3):
        for b in range(3):
            for c in range(3):
                tap = 9 * a + 3 * b + c
                moved_src = jnp.roll(source_f, (1 - a, 1 - b, 1 - c), axis=(1, 2, 3)).reshape(channels, -1)
                pieces.append(lax.dot_general(slope_flat, moved_src, (((1,), (1,)), ((), ())), precision=lax.Precision.HIGHEST, preferred_element_type=jnp.float32))
                moved_slope = jnp.roll(slope_f, (a - 1, b - 1, c - 1), axis=(1, 2, 3)).reshape(channels, -1)
                grad_source = grad_source + jnp.dot(kernel_f[tap].T, moved_slope, precision=lax.Precision.HIGHEST, preferred_element_type=jnp.float32)
    total_cells = source.shape[1] * source.shape[2] * source.shape[3]
    grad_kernel = jnp.stack(pieces, axis=0).reshape(-1) / jnp.sqrt(jnp.float32(total_cells))
    return (grad_source.reshape(source.shape).astype(jnp.bfloat16), grad_kernel)
```

```python
import math

import jax
import jax.numpy as jnp
from jax import lax
from jax.experimental import pallas as pl
from jax.experimental.pallas import tpu as pltpu
from jax.sharding import PartitionSpec as P

MESH = pl.DeviceIdType.MESH
F32, BF16 = jnp.float32, jnp.bfloat16
C, NZ = 64, 128
WX, WY = 2, 8
DEPTH = 8
ROWS = 27
OWN = 432
CELLS = 32 * 128 * 128
NT = (((1,), (1,)), ((), ()))


def spot(y, x, core, z):
    return (
        (y * 2 + lax.div(x, 2)) * 2 + core,
        lax.rem(x, 2) * DEPTH + z,
    )


def body(
    source, preact, cotangent, kernel, gs_out, gk_out,
    pv, cv, sv, kv, wide, wide_src, wide_out, slope, src3, weights, prod_lo, prod_hi,
    part, core_in, half, a_in, quarter, b_in, last, z_out, z_in,
    load_sem, halo_send, halo_recv, core_send, core_recv, a_send, a_recv, b_send, b_recv, z_send, z_recv,
):
    gx, gy = lax.axis_index("gx"), lax.axis_index("gy")
    core, xhi, y = lax.rem(gx, 2), lax.rem(lax.div(gx, 2), 2), lax.div(gx, 4)
    xlo, z = lax.div(gy, DEPTH), lax.rem(gy, DEPTH)
    x = xhi * 2 + xlo
    other = 1 - core

    up_x, dn_x = lax.rem(gx + 1, 16), lax.rem(gx + 15, 16)
    up_y, dn_y = lax.rem(gy + 1, 16), lax.rem(gy + 15, 16)

    loads = [
        pltpu.make_async_copy(src, dst, load_sem.at[n])
        for n, (src, dst) in enumerate(((preact, pv), (cotangent, cv), (source, sv), (kernel, kv)))
    ]
    for copy in loads:
        copy.start()

    a_to, b_to, z_to = [], [], []
    for k in (1, 2, 3):
        a_to.append(spot(lax.rem(y + k * other, 4), lax.rem(x + k * core, 4), core, z))
        b_to.append(spot(lax.rem(y + k * core, 4), lax.rem(x + k * other, 4), core, z))
    for k in range(1, DEPTH):
        z_to.append(spot(y, x, core, lax.rem(z + k, DEPTH)))
    sides = [
        (up_x, gy), (dn_x, gy), (gx, up_y), (gx, dn_y),
        (up_x, up_y), (up_x, dn_y), (dn_x, up_y), (dn_x, dn_y),
    ]
    partner = spot(y, x, other, z)
    everyone = sides + [partner] + a_to + b_to + z_to
    barrier = pltpu.get_barrier_semaphore()
    for device in everyone:
        pl.semaphore_signal(barrier, inc=1, device_id=device, device_id_type=MESH)

    loads[0].wait()
    loads[1].wait()
    for c in range(0, C, 8):
        keep = pv[c : c + 8].astype(F32) > 0
        masked = jnp.where(keep, cv[c : c + 8].astype(F32), 0.0)
        wide[c * 16 : c * 16 + 128, :] = masked.reshape(128, NZ)
    for i in range(WX):
        for j in range(WY):
            slope[i + 1, j + 1] = wide[pl.ds(i * WY + j, C, stride=WX * WY), :].astype(BF16)

    pl.semaphore_wait(barrier, len(everyone))
    ends = [
        (slope.at[2, 1:9], slope.at[0, 1:9]),
        (slope.at[1, 1:9], slope.at[3, 1:9]),
        (slope.at[1:3, 8], slope.at[1:3, 0]),
        (slope.at[1:3, 1], slope.at[1:3, 9]),
        (slope.at[2, 8], slope.at[0, 0]),
        (slope.at[2, 1], slope.at[0, 9]),
        (slope.at[1, 8], slope.at[3, 0]),
        (slope.at[1, 1], slope.at[3, 9]),
    ]
    halos = []
    for n, ((src, dst), device) in enumerate(zip(ends, sides)):
        copy = pltpu.make_async_remote_copy(
            src, dst, halo_send.at[n], halo_recv.at[n], device_id=device, device_id_type=MESH
        )
        copy.start()
        halos.append(copy)

    loads[2].wait()
    for c in range(0, C, 8):
        wide_src[c * 16 : c * 16 + 128, :] = sv[c : c + 8].astype(F32).reshape(128, NZ)
    for i in range(WX):
        for j in range(WY):
            block = wide_src[pl.ds(i * WY + j, C, stride=WX * WY), :]
            for c, shift in enumerate((1, 0, NZ - 1)):
                moved = pltpu.roll(block, shift, 1) if shift else block
                src3[i, j // 2, c * C : (c + 1) * C, (j % 2) * NZ : (j % 2 + 1) * NZ] = moved.astype(BF16)
    loads[3].wait()
    for c in range(3):
        for ab in range(0, 9, 2):
            taps = [kv[3 * n + c].astype(F32) for n in range(ab, min(ab + 2, 9))]
            pair = jnp.concatenate(taps, axis=0) if len(taps) > 1 else taps[0]
            weights[c * C : (c + 1) * C, ab * C : (ab + len(taps)) * C] = pair.T.astype(BF16)

    for copy in halos:
        copy.wait_recv()

    def columns(a, b, i, jp):
        return jnp.concatenate([slope[i + 2 - a, 2 * jp + 2 - b], slope[i + 2 - a, 2 * jp + 3 - b]], axis=1)

    sends = []
    for a in range(3):
        total = None
        for i in range(WX):
            for jp in range(WY // 2):
                left = jnp.concatenate([columns(a, b, i, jp) for b in range(3)], axis=0)
                term = lax.dot_general(left, src3[i, jp], NT, preferred_element_type=F32)
                total = term if total is None else total + term
        prod_lo[a * 192 : (a + 1) * 192, :] = total[:, :128]
        prod_hi[a * 192 : (a + 1) * 192, 0:C] = total[:, 128:]
        for b in range(3):
            base = (a * 3 + b) * C
            lo = [prod_lo[pl.ds(base + odd, 32, stride=2), :] for odd in (0, 1)]
            hi = [prod_hi[pl.ds(base + odd, 32, stride=2), :] for odd in (0, 1)]
            pairs = (
                jnp.concatenate([lo[0][:, :C], lo[1][:, :C]], axis=1),
                jnp.concatenate([lo[0][:, C:], lo[1][:, C:]], axis=1),
                jnp.concatenate([hi[0][:, :C], hi[1][:, :C]], axis=1),
            )
            for c, rows in enumerate(pairs):
                start = 32 * ((a * 3 + b) * 3 + c)
                at = start
                while at < start + 32:
                    q, r = divmod(at, ROWS)
                    count = min(ROWS - r, start + 32 - at)
                    part[(q >> 1) & 1, q >> 3, ((q >> 2) & 1) * 2 + (q & 1), r : r + count, :] = (
                        rows[at - start : at - start + count, :]
                    )
                    at += count
        for n in ((0,), (1,), (2, 3))[a]:
            copy = pltpu.make_async_remote_copy(
                part.at[other, n], core_in.at[n], core_send.at[n], core_recv.at[n],
                device_id=partner, device_id_type=MESH,
            )
            copy.start()
            sends.append(copy)

    def data_gradient(i):
        for jp in range(WY // 2):
            right = jnp.concatenate([columns(a, b, i, jp) for a in range(3) for b in range(3)], axis=0)
            out = jnp.dot(weights[...], right, preferred_element_type=F32)
            for half_at in range(2):
                three = [
                    out[c * C : (c + 1) * C, half_at * NZ : (half_at + 1) * NZ] for c in range(3)
                ]
                whole = pltpu.roll(three[0], NZ - 1, 1) + three[1] + pltpu.roll(three[2], 1, 1)
                wide_out[pl.ds(i * WY + 2 * jp + half_at, C, stride=WX * WY), :] = whole

    data_gradient(0)

    a_me = y * other + x * core
    b_me = x * other + y * core
    for n in range(4):
        sends[n].wait_recv()
        for m in range(4):
            at = (n * other + m * core) * 4 + m * other + n * core
            half[at] = part[core, n, m] + core_in[n, m]
    a_copies = []
    for k in (1, 2, 3):
        copy = pltpu.make_async_remote_copy(
            half.at[pl.ds(lax.rem(a_me + k, 4) * 4, 4)], a_in.at[k - 1], a_send.at[k - 1], a_recv.at[k - 1],
            device_id=a_to[k - 1], device_id_type=MESH,
        )
        copy.start()
        a_copies.append(copy)

    data_gradient(1)

    for copy in a_copies:
        copy.wait_recv()
    for m in range(4):
        quarter[m] = half[a_me * 4 + m] + a_in[0, m] + a_in[1, m] + a_in[2, m]
    b_copies = []
    for k in (1, 2, 3):
        copy = pltpu.make_async_remote_copy(
            quarter.at[lax.rem(b_me + k, 4)], b_in.at[k - 1], b_send.at[k - 1], b_recv.at[k - 1],
            device_id=b_to[k - 1], device_id_type=MESH,
        )
        copy.start()
        b_copies.append(copy)

    for c in range(0, C, 8):
        gs_out[c : c + 8] = wide_out[c * 16 : c * 16 + 128, :].reshape(8, WX, WY, NZ).astype(BF16)

    for copy in b_copies:
        copy.wait_recv()
    last[...] = quarter[b_me] + b_in[0] + b_in[1] + b_in[2]
    lane = lax.broadcasted_iota(jnp.int32, (8, NZ), 1)
    for n in range(DEPTH):
        row, off = divmod(n * OWN, NZ)
        lower = last[row : row + 8, :]
        upper = last[row + 1 : row + 9, :]
        if off:
            lower = jnp.where(lane < NZ - off, pltpu.roll(lower, NZ - off, 1), pltpu.roll(upper, NZ - off, 1))
        z_out[n] = lower
    z_copies = []
    for k in range(1, DEPTH):
        copy = pltpu.make_async_remote_copy(
            z_out.at[lax.rem(z + k, DEPTH)], z_in.at[k - 1], z_send.at[k - 1], z_recv.at[k - 1],
            device_id=z_to[k - 1], device_id_type=MESH,
        )
        copy.start()
        z_copies.append(copy)
    for copy in z_copies:
        copy.wait_recv()
    mine = z_out[z]
    for k in range(DEPTH - 1):
        mine = mine + z_in[k]
    gk_out[...] = mine * (1.0 / math.sqrt(CELLS))

    for copy in halos + sends + a_copies + b_copies + z_copies:
        copy.wait_send()


def on_device(source, preact, cotangent, kernel):
    dma = pltpu.SemaphoreType.DMA
    blocks = (WX + 2, WY + 2, C, NZ)
    grad_source, grad_kernel = pl.pallas_call(
        body,
        out_shape=(
            jax.ShapeDtypeStruct(source.shape, BF16),
            jax.ShapeDtypeStruct((8, NZ), F32),
        ),
        in_specs=[pl.BlockSpec(memory_space=pl.ANY)] * 4,
        out_specs=(pl.BlockSpec(memory_space=pltpu.VMEM), pl.BlockSpec(memory_space=pltpu.VMEM)),
        scratch_shapes=[
            pltpu.VMEM(source.shape, BF16),
            pltpu.VMEM(source.shape, BF16),
            pltpu.VMEM(source.shape, BF16),
            pltpu.VMEM(kernel.shape, BF16),
            pltpu.VMEM((C * WX * WY, NZ), F32),
            pltpu.VMEM((C * WX * WY, NZ), F32),
            pltpu.VMEM((C * WX * WY, NZ), F32),
            pltpu.VMEM(blocks, BF16),
            pltpu.VMEM((WX, WY // 2, 3 * C, 2 * NZ), BF16),
            pltpu.VMEM((3 * C, 9 * C), BF16),
            pltpu.VMEM((9 * C, NZ), F32),
            pltpu.VMEM((9 * C, NZ), F32),
            pltpu.VMEM((2, 4, 4, 32, NZ), F32),
            pltpu.VMEM((4, 4, 32, NZ), F32),
            pltpu.VMEM((16, 32, NZ), F32),
            pltpu.VMEM((3, 4, 32, NZ), F32),
            pltpu.VMEM((4, 32, NZ), F32),
            pltpu.VMEM((3, 32, NZ), F32),
            pltpu.VMEM((32, NZ), F32),
            pltpu.VMEM((8, 8, NZ), F32),
            pltpu.VMEM((7, 8, NZ), F32),
            dma((4,)),
            dma((8,)), dma((8,)), dma((4,)), dma((4,)), dma((3,)), dma((3,)),
            dma((3,)), dma((3,)), dma((7,)), dma((7,)),
        ],
        compiler_params=pltpu.CompilerParams(collective_id=0, has_side_effects=True),
    )(source, preact, cotangent, kernel)
    return grad_source, grad_kernel.reshape(-1)[:OWN]


def solution(mesh):
    placed = (P(None, "gx", "gy", None), P(None, "gx", "gy", None), P(None, "gx", "gy", None), P())
    return jax.shard_map(
        on_device,
        mesh=mesh,
        in_specs=placed,
        out_specs=(P(None, "gx", "gy", None), P(("gx", "gy"))),
        check_vma=False,
    )
```

```python
import math

import jax
import jax.numpy as jnp
from jax import lax
from jax.experimental import pallas as pl
from jax.experimental.pallas import tpu as pltpu
from jax.sharding import PartitionSpec as P

MESH = pl.DeviceIdType.MESH
F32, BF16 = jnp.float32, jnp.bfloat16
C, NZ = 64, 128
WX, WY = 2, 8
DEPTH = 8
ROWS = 27
OWN = 432
PLANE = sorted(
    ((dy, dx) for dy in range(4) for dx in range(4) if dy or dx),
    key=lambda d: -min(d[0], 4 - d[0]) - min(d[1], 4 - d[1]),
)
CELLS = 32 * 128 * 128
NT = (((1,), (1,)), ((), ()))


def spot(y, x, core, z):
    return (
        (y * 2 + lax.div(x, 2)) * 2 + core,
        lax.rem(x, 2) * DEPTH + z,
    )


def body(
    source, preact, cotangent, kernel, gs_out, gk_out,
    pv, cv, sv, kv, wide, wide_src, wide_out, slope, src3, weights, prod_lo, prod_hi,
    part, core_in, half, plane_in, last, z_out, z_in,
    load_sem, halo_send, halo_recv, core_send, core_recv, plane_send, plane_recv, z_send, z_recv,
):
    gx, gy = lax.axis_index("gx"), lax.axis_index("gy")
    core, xhi, y = lax.rem(gx, 2), lax.rem(lax.div(gx, 2), 2), lax.div(gx, 4)
    xlo, z = lax.div(gy, DEPTH), lax.rem(gy, DEPTH)
    x = xhi * 2 + xlo
    other = 1 - core

    up_x, dn_x = lax.rem(gx + 1, 16), lax.rem(gx + 15, 16)
    up_y, dn_y = lax.rem(gy + 1, 16), lax.rem(gy + 15, 16)

    loads = [
        pltpu.make_async_copy(src, dst, load_sem.at[n])
        for n, (src, dst) in enumerate(((preact, pv), (cotangent, cv), (source, sv), (kernel, kv)))
    ]
    for copy in loads:
        copy.start()

    plane_at, plane_to, z_to = [], [], []
    for dy, dx in PLANE:
        to_y, to_x = lax.rem(y + dy, 4), lax.rem(x + dx, 4)
        plane_at.append(to_y * 4 + to_x)
        plane_to.append(spot(to_y, to_x, core, z))
    for k in range(1, DEPTH):
        z_to.append(spot(y, x, core, lax.rem(z + k, DEPTH)))
    sides = [
        (up_x, gy), (dn_x, gy), (gx, up_y), (gx, dn_y),
        (up_x, up_y), (up_x, dn_y), (dn_x, up_y), (dn_x, dn_y),
    ]
    partner = spot(y, x, other, z)
    everyone = sides + [partner] + plane_to + z_to
    barrier = pltpu.get_barrier_semaphore()
    for device in everyone:
        pl.semaphore_signal(barrier, inc=1, device_id=device, device_id_type=MESH)

    loads[0].wait()
    loads[1].wait()
    for c in range(0, C, 8):
        keep = pv[c : c + 8].astype(F32) > 0
        masked = jnp.where(keep, cv[c : c + 8].astype(F32), 0.0)
        wide[c * 16 : c * 16 + 128, :] = masked.reshape(128, NZ)
    for i in range(WX):
        for j in range(WY):
            slope[i + 1, j + 1] = wide[pl.ds(i * WY + j, C, stride=WX * WY), :].astype(BF16)

    pl.semaphore_wait(barrier, len(everyone))
    ends = [
        (slope.at[2, 1:9], slope.at[0, 1:9]),
        (slope.at[1, 1:9], slope.at[3, 1:9]),
        (slope.at[1:3, 8], slope.at[1:3, 0]),
        (slope.at[1:3, 1], slope.at[1:3, 9]),
        (slope.at[2, 8], slope.at[0, 0]),
        (slope.at[2, 1], slope.at[0, 9]),
        (slope.at[1, 8], slope.at[3, 0]),
        (slope.at[1, 1], slope.at[3, 9]),
    ]
    halos = []
    for n, ((src, dst), device) in enumerate(zip(ends, sides)):
        copy = pltpu.make_async_remote_copy(
            src, dst, halo_send.at[n], halo_recv.at[n], device_id=device, device_id_type=MESH
        )
        copy.start()
        halos.append(copy)

    loads[2].wait()
    for c in range(0, C, 8):
        wide_src[c * 16 : c * 16 + 128, :] = sv[c : c + 8].astype(F32).reshape(128, NZ)
    for i in range(WX):
        for j in range(WY):
            block = wide_src[pl.ds(i * WY + j, C, stride=WX * WY), :]
            for c, shift in enumerate((1, 0, NZ - 1)):
                moved = pltpu.roll(block, shift, 1) if shift else block
                src3[i, j // 2, c * C : (c + 1) * C, (j % 2) * NZ : (j % 2 + 1) * NZ] = moved.astype(BF16)
    loads[3].wait()
    for c in range(3):
        for ab in range(0, 9, 2):
            taps = [kv[3 * n + c].astype(F32) for n in range(ab, min(ab + 2, 9))]
            pair = jnp.concatenate(taps, axis=0) if len(taps) > 1 else taps[0]
            weights[c * C : (c + 1) * C, ab * C : (ab + len(taps)) * C] = pair.T.astype(BF16)

    for copy in halos:
        copy.wait_recv()

    def columns(a, b, i, jp):
        return jnp.concatenate([slope[i + 2 - a, 2 * jp + 2 - b], slope[i + 2 - a, 2 * jp + 3 - b]], axis=1)

    sends = []
    for a in range(3):
        total = None
        for i in range(WX):
            for jp in range(WY // 2):
                left = jnp.concatenate([columns(a, b, i, jp) for b in range(3)], axis=0)
                term = lax.dot_general(left, src3[i, jp], NT, preferred_element_type=F32)
                total = term if total is None else total + term
        prod_lo[a * 192 : (a + 1) * 192, :] = total[:, :128]
        prod_hi[a * 192 : (a + 1) * 192, 0:C] = total[:, 128:]
        for b in range(3):
            base = (a * 3 + b) * C
            lo = [prod_lo[pl.ds(base + odd, 32, stride=2), :] for odd in (0, 1)]
            hi = [prod_hi[pl.ds(base + odd, 32, stride=2), :] for odd in (0, 1)]
            pairs = (
                jnp.concatenate([lo[0][:, :C], lo[1][:, :C]], axis=1),
                jnp.concatenate([lo[0][:, C:], lo[1][:, C:]], axis=1),
                jnp.concatenate([hi[0][:, :C], hi[1][:, :C]], axis=1),
            )
            for c, rows in enumerate(pairs):
                start = 32 * ((a * 3 + b) * 3 + c)
                at = start
                while at < start + 32:
                    q, r = divmod(at, ROWS)
                    count = min(ROWS - r, start + 32 - at)
                    part[(q >> 1) & 1, q >> 3, ((q >> 2) & 1) * 2 + (q & 1), r : r + count, :] = (
                        rows[at - start : at - start + count, :]
                    )
                    at += count
        for n in ((0,), (1,), (2, 3))[a]:
            copy = pltpu.make_async_remote_copy(
                part.at[other, n], core_in.at[n], core_send.at[n], core_recv.at[n],
                device_id=partner, device_id_type=MESH,
            )
            copy.start()
            sends.append(copy)

    def data_gradient(i):
        for jp in range(WY // 2):
            right = jnp.concatenate([columns(a, b, i, jp) for a in range(3) for b in range(3)], axis=0)
            out = jnp.dot(weights[...], right, preferred_element_type=F32)
            for half_at in range(2):
                three = [
                    out[c * C : (c + 1) * C, half_at * NZ : (half_at + 1) * NZ] for c in range(3)
                ]
                whole = pltpu.roll(three[0], NZ - 1, 1) + three[1] + pltpu.roll(three[2], 1, 1)
                wide_out[pl.ds(i * WY + 2 * jp + half_at, C, stride=WX * WY), :] = whole

    data_gradient(0)

    for n in range(4):
        sends[n].wait_recv()
        for m in range(4):
            half[n * 4 + m] = (part[core, n, m] + core_in[n, m]).astype(BF16)
    plane_copies = []
    for k, (at, device) in enumerate(zip(plane_at, plane_to)):
        copy = pltpu.make_async_remote_copy(
            half.at[at], plane_in.at[k], plane_send.at[k], plane_recv.at[k],
            device_id=device, device_id_type=MESH,
        )
        copy.start()
        plane_copies.append(copy)

    data_gradient(1)
    for c in range(0, C, 8):
        gs_out[c : c + 8] = wide_out[c * 16 : c * 16 + 128, :].reshape(8, WX, WY, NZ).astype(BF16)

    total = part[core, y, x] + core_in[y, x]
    for k in reversed(range(len(PLANE))):
        plane_copies[k].wait_recv()
        total = total + plane_in[k].astype(F32)
    last[...] = total
    lane = lax.broadcasted_iota(jnp.int32, (8, NZ), 1)
    for n in range(DEPTH):
        row, off = divmod(n * OWN, NZ)
        lower = last[row : row + 8, :]
        upper = last[row + 1 : row + 9, :]
        if off:
            lower = jnp.where(lane < NZ - off, pltpu.roll(lower, NZ - off, 1), pltpu.roll(upper, NZ - off, 1))
        z_out[n] = lower
    z_copies = []
    for k in range(1, DEPTH):
        copy = pltpu.make_async_remote_copy(
            z_out.at[lax.rem(z + k, DEPTH)], z_in.at[k - 1], z_send.at[k - 1], z_recv.at[k - 1],
            device_id=z_to[k - 1], device_id_type=MESH,
        )
        copy.start()
        z_copies.append(copy)
    for copy in z_copies:
        copy.wait_recv()
    mine = z_out[z]
    for k in range(DEPTH - 1):
        mine = mine + z_in[k]
    gk_out[...] = mine * (1.0 / math.sqrt(CELLS))

    for copy in halos + sends + plane_copies + z_copies:
        copy.wait_send()


def on_device(source, preact, cotangent, kernel):
    dma = pltpu.SemaphoreType.DMA
    blocks = (WX + 2, WY + 2, C, NZ)
    grad_source, grad_kernel = pl.pallas_call(
        body,
        out_shape=(
            pltpu.VMEM(source.shape, BF16),
            pltpu.VMEM((8, NZ), F32),
        ),
        in_specs=[pl.BlockSpec(memory_space=pl.ANY)] * 4,
        out_specs=(pl.BlockSpec(memory_space=pltpu.VMEM), pl.BlockSpec(memory_space=pltpu.VMEM)),
        scratch_shapes=[
            pltpu.VMEM(source.shape, BF16),
            pltpu.VMEM(source.shape, BF16),
            pltpu.VMEM(source.shape, BF16),
            pltpu.VMEM(kernel.shape, BF16),
            pltpu.VMEM((C * WX * WY, NZ), F32),
            pltpu.VMEM((C * WX * WY, NZ), F32),
            pltpu.VMEM((C * WX * WY, NZ), F32),
            pltpu.VMEM(blocks, BF16),
            pltpu.VMEM((WX, WY // 2, 3 * C, 2 * NZ), BF16),
            pltpu.VMEM((3 * C, 9 * C), BF16),
            pltpu.VMEM((9 * C, NZ), F32),
            pltpu.VMEM((9 * C, NZ), F32),
            pltpu.VMEM((2, 4, 4, 32, NZ), F32),
            pltpu.VMEM((4, 4, 32, NZ), F32),
            pltpu.VMEM((16, 32, NZ), BF16),
            pltpu.VMEM((15, 32, NZ), BF16),
            pltpu.VMEM((32, NZ), F32),
            pltpu.VMEM((8, 8, NZ), F32),
            pltpu.VMEM((7, 8, NZ), F32),
            dma((4,)),
            dma((8,)), dma((8,)), dma((4,)), dma((4,)), dma((15,)), dma((15,)),
            dma((7,)), dma((7,)),
        ],
        compiler_params=pltpu.CompilerParams(collective_id=0, has_side_effects=True),
    )(source, preact, cotangent, kernel)
    return grad_source, grad_kernel.reshape(-1)[:OWN]


def solution(mesh):
    placed = (P(None, "gx", "gy", None), P(None, "gx", "gy", None), P(None, "gx", "gy", None), P())
    return jax.shard_map(
        on_device,
        mesh=mesh,
        in_specs=placed,
        out_specs=(P(None, "gx", "gy", None), P(("gx", "gy"))),
        check_vma=False,
    )
```

```python
import math

import jax
import jax.numpy as jnp
from jax import lax
from jax.experimental import pallas as pl
from jax.experimental.pallas import tpu as pltpu
from jax.sharding import PartitionSpec as P

MESH = pl.DeviceIdType.MESH
F32, BF16 = jnp.float32, jnp.bfloat16
C, NZ = 64, 128
WX, WY = 2, 8
DEPTH = 8
ROWS = 27
OWN = 432
PLANE = sorted(
    ((dy, dx) for dy in range(4) for dx in range(4) if dy or dx),
    key=lambda d: -min(d[0], 4 - d[0]) - min(d[1], 4 - d[1]),
)
CELLS = 32 * 128 * 128
NT = (((1,), (1,)), ((), ()))


def spot(y, x, core, z):
    return (
        (y * 2 + lax.div(x, 2)) * 2 + core,
        lax.rem(x, 2) * DEPTH + z,
    )


def body(
    source, preact, cotangent, kernel, gs_out, gk_out,
    pv, cv, sv, kv, wide, wide_src, wide_out, slope, src3, weights, prod_lo, prod_hi,
    part, core_in, half, plane_in, last, z_out, z_in,
    load_sem, halo_send, halo_recv, core_send, core_recv, plane_send, plane_recv, z_send, z_recv,
):
    gx, gy = lax.axis_index("gx"), lax.axis_index("gy")
    core, xhi, y = lax.rem(gx, 2), lax.rem(lax.div(gx, 2), 2), lax.div(gx, 4)
    xlo, z = lax.div(gy, DEPTH), lax.rem(gy, DEPTH)
    x = xhi * 2 + xlo
    other = 1 - core

    up_x, dn_x = lax.rem(gx + 1, 16), lax.rem(gx + 15, 16)
    up_y, dn_y = lax.rem(gy + 1, 16), lax.rem(gy + 15, 16)

    loads = [
        pltpu.make_async_copy(src, dst, load_sem.at[n])
        for n, (src, dst) in enumerate(((preact, pv), (cotangent, cv), (source, sv), (kernel, kv)))
    ]
    for copy in loads:
        copy.start()

    plane_at, plane_to, z_to = [], [], []
    for dy, dx in PLANE:
        to_y, to_x = lax.rem(y + dy, 4), lax.rem(x + dx, 4)
        plane_at.append(to_y * 4 + to_x)
        plane_to.append(spot(to_y, to_x, core, z))
    for k in range(1, DEPTH):
        z_to.append(spot(y, x, core, lax.rem(z + k, DEPTH)))
    sides = [
        (up_x, gy), (dn_x, gy), (gx, up_y), (gx, dn_y),
        (up_x, up_y), (up_x, dn_y), (dn_x, up_y), (dn_x, dn_y),
    ]
    partner = spot(y, x, other, z)
    everyone = sides + [partner] + plane_to + z_to
    barrier = pltpu.get_barrier_semaphore()
    for device in everyone:
        pl.semaphore_signal(barrier, inc=1, device_id=device, device_id_type=MESH)

    loads[0].wait()
    loads[1].wait()
    for c in range(0, C, 8):
        keep = pv[c : c + 8].astype(F32) > 0
        masked = jnp.where(keep, cv[c : c + 8].astype(F32), 0.0)
        wide[c * 16 : c * 16 + 128, :] = masked.reshape(128, NZ)
    for i in range(WX):
        for j in range(WY):
            slope[i + 1, j + 1] = wide[pl.ds(i * WY + j, C, stride=WX * WY), :].astype(BF16)

    pl.semaphore_wait(barrier, len(everyone))
    ends = [
        (slope.at[2, 1:9], slope.at[0, 1:9]),
        (slope.at[1, 1:9], slope.at[3, 1:9]),
        (slope.at[1:3, 8], slope.at[1:3, 0]),
        (slope.at[1:3, 1], slope.at[1:3, 9]),
        (slope.at[2, 8], slope.at[0, 0]),
        (slope.at[2, 1], slope.at[0, 9]),
        (slope.at[1, 8], slope.at[3, 0]),
        (slope.at[1, 1], slope.at[3, 9]),
    ]
    halos = []
    for n, ((src, dst), device) in enumerate(zip(ends, sides)):
        copy = pltpu.make_async_remote_copy(
            src, dst, halo_send.at[n], halo_recv.at[n], device_id=device, device_id_type=MESH
        )
        copy.start()
        halos.append(copy)

    loads[2].wait()
    for c in range(0, C, 8):
        wide_src[c * 16 : c * 16 + 128, :] = sv[c : c + 8].astype(F32).reshape(128, NZ)
    for i in range(WX):
        for j in range(WY):
            block = wide_src[pl.ds(i * WY + j, C, stride=WX * WY), :]
            for c, shift in enumerate((1, 0, NZ - 1)):
                moved = pltpu.roll(block, shift, 1) if shift else block
                src3[i, j // 2, c * C : (c + 1) * C, (j % 2) * NZ : (j % 2 + 1) * NZ] = moved.astype(BF16)
    loads[3].wait()
    for c in range(3):
        for ab in range(0, 9, 2):
            taps = [kv[3 * n + c].astype(F32) for n in range(ab, min(ab + 2, 9))]
            pair = jnp.concatenate(taps, axis=0) if len(taps) > 1 else taps[0]
            weights[c * C : (c + 1) * C, ab * C : (ab + len(taps)) * C] = pair.T.astype(BF16)

    def columns(a, b, i, jp):
        return jnp.concatenate([slope[i + 2 - a, 2 * jp + 2 - b], slope[i + 2 - a, 2 * jp + 3 - b]], axis=1)

    sends = []
    for a in (1, 0, 2):
        for n in ((1, 6, 7), (2, 3), (0, 4, 5))[a]:
            halos[n].wait_recv()
        total = None
        for i in range(WX):
            for jp in range(WY // 2):
                left = jnp.concatenate([columns(a, b, i, jp) for b in range(3)], axis=0)
                term = lax.dot_general(left, src3[i, jp], NT, preferred_element_type=F32)
                total = term if total is None else total + term
        prod_lo[a * 192 : (a + 1) * 192, :] = total[:, :128]
        prod_hi[a * 192 : (a + 1) * 192, 0:C] = total[:, 128:]
        for b in range(3):
            base = (a * 3 + b) * C
            lo = [prod_lo[pl.ds(base + odd, 32, stride=2), :] for odd in (0, 1)]
            hi = [prod_hi[pl.ds(base + odd, 32, stride=2), :] for odd in (0, 1)]
            pairs = (
                jnp.concatenate([lo[0][:, :C], lo[1][:, :C]], axis=1),
                jnp.concatenate([lo[0][:, C:], lo[1][:, C:]], axis=1),
                jnp.concatenate([hi[0][:, :C], hi[1][:, :C]], axis=1),
            )
            for c, rows in enumerate(pairs):
                start = 32 * ((a * 3 + b) * 3 + c)
                at = start
                while at < start + 32:
                    q, r = divmod(at, ROWS)
                    count = min(ROWS - r, start + 32 - at)
                    part[(q >> 1) & 1, q >> 3, ((q >> 2) & 1) * 2 + (q & 1), r : r + count, :] = (
                        rows[at - start : at - start + count, :]
                    )
                    at += count
        for n in ((0, 1), (), (2, 3))[a]:
            copy = pltpu.make_async_remote_copy(
                part.at[other, n], core_in.at[n], core_send.at[n], core_recv.at[n],
                device_id=partner, device_id_type=MESH,
            )
            copy.start()
            sends.append(copy)

    def data_gradient(i):
        for jp in range(WY // 2):
            right = jnp.concatenate([columns(a, b, i, jp) for a in range(3) for b in range(3)], axis=0)
            out = jnp.dot(weights[...], right, preferred_element_type=F32)
            for half_at in range(2):
                three = [
                    out[c * C : (c + 1) * C, half_at * NZ : (half_at + 1) * NZ] for c in range(3)
                ]
                whole = pltpu.roll(three[0], NZ - 1, 1) + three[1] + pltpu.roll(three[2], 1, 1)
                wide_out[pl.ds(i * WY + 2 * jp + half_at, C, stride=WX * WY), :] = whole

    data_gradient(0)

    for n in range(4):
        sends[n].wait_recv()
        for m in range(4):
            half[n * 4 + m] = (part[core, n, m] + core_in[n, m]).astype(BF16)
    plane_copies = []
    for k, (at, device) in enumerate(zip(plane_at, plane_to)):
        copy = pltpu.make_async_remote_copy(
            half.at[at], plane_in.at[k], plane_send.at[k], plane_recv.at[k],
            device_id=device, device_id_type=MESH,
        )
        copy.start()
        plane_copies.append(copy)

    data_gradient(1)
    for c in range(0, C, 8):
        gs_out[c : c + 8] = wide_out[c * 16 : c * 16 + 128, :].reshape(8, WX, WY, NZ).astype(BF16)

    total = part[core, y, x] + core_in[y, x]
    for k in reversed(range(len(PLANE))):
        plane_copies[k].wait_recv()
        total = total + plane_in[k].astype(F32)
    last[...] = total
    lane = lax.broadcasted_iota(jnp.int32, (8, NZ), 1)
    for n in range(DEPTH):
        row, off = divmod(n * OWN, NZ)
        lower = last[row : row + 8, :]
        upper = last[row + 1 : row + 9, :]
        if off:
            lower = jnp.where(lane < NZ - off, pltpu.roll(lower, NZ - off, 1), pltpu.roll(upper, NZ - off, 1))
        z_out[n] = lower
    z_copies = []
    for k in range(1, DEPTH):
        copy = pltpu.make_async_remote_copy(
            z_out.at[lax.rem(z + k, DEPTH)], z_in.at[k - 1], z_send.at[k - 1], z_recv.at[k - 1],
            device_id=z_to[k - 1], device_id_type=MESH,
        )
        copy.start()
        z_copies.append(copy)
    for copy in z_copies:
        copy.wait_recv()
    mine = z_out[z]
    for k in range(DEPTH - 1):
        mine = mine + z_in[k]
    mine = mine * (1.0 / math.sqrt(CELLS))
    for row in range(0, OWN, NZ):
        count = min(NZ, OWN - row)
        gk_out[row : row + count] = mine[row // NZ, :count]

    for copy in halos + sends + plane_copies + z_copies:
        copy.wait_send()


def on_device(source, preact, cotangent, kernel):
    dma = pltpu.SemaphoreType.DMA
    blocks = (WX + 2, WY + 2, C, NZ)
    grad_source, grad_kernel = pl.pallas_call(
        body,
        out_shape=(
            pltpu.VMEM(source.shape, BF16),
            pltpu.VMEM((OWN,), F32),
        ),
        in_specs=[pl.BlockSpec(memory_space=pl.ANY)] * 4,
        out_specs=(pl.BlockSpec(memory_space=pltpu.VMEM), pl.BlockSpec(memory_space=pltpu.VMEM)),
        scratch_shapes=[
            pltpu.VMEM(source.shape, BF16),
            pltpu.VMEM(source.shape, BF16),
            pltpu.VMEM(source.shape, BF16),
            pltpu.VMEM(kernel.shape, BF16),
            pltpu.VMEM((C * WX * WY, NZ), F32),
            pltpu.VMEM((C * WX * WY, NZ), F32),
            pltpu.VMEM((C * WX * WY, NZ), F32),
            pltpu.VMEM(blocks, BF16),
            pltpu.VMEM((WX, WY // 2, 3 * C, 2 * NZ), BF16),
            pltpu.VMEM((3 * C, 9 * C), BF16),
            pltpu.VMEM((9 * C, NZ), F32),
            pltpu.VMEM((9 * C, NZ), F32),
            pltpu.VMEM((2, 4, 4, 32, NZ), F32),
            pltpu.VMEM((4, 4, 32, NZ), F32),
            pltpu.VMEM((16, 32, NZ), BF16),
            pltpu.VMEM((15, 32, NZ), BF16),
            pltpu.VMEM((32, NZ), F32),
            pltpu.VMEM((8, 8, NZ), F32),
            pltpu.VMEM((7, 8, NZ), F32),
            dma((4,)),
            dma((8,)), dma((8,)), dma((4,)), dma((4,)), dma((15,)), dma((15,)),
            dma((7,)), dma((7,)),
        ],
        compiler_params=pltpu.CompilerParams(collective_id=0, has_side_effects=True),
    )(source, preact, cotangent, kernel)
    return grad_source, grad_kernel


def solution(mesh):
    placed = (P(None, "gx", "gy", None), P(None, "gx", "gy", None), P(None, "gx", "gy", None), P())
    return jax.shard_map(
        on_device,
        mesh=mesh,
        in_specs=placed,
        out_specs=(P(None, "gx", "gy", None), P(("gx", "gy"))),
        check_vma=False,
    )
```

```python
import math

import jax
import jax.numpy as jnp
from jax import lax
from jax.experimental import pallas as pl
from jax.experimental.pallas import tpu as pltpu
from jax.sharding import PartitionSpec as P

MESH = pl.DeviceIdType.MESH
F32, BF16 = jnp.float32, jnp.bfloat16
C, NZ = 64, 128
WX, WY = 2, 8
DEPTH = 8
ROWS = 27
OWN = 432
PLANE = sorted(
    ((dy, dx, dc) for dy in range(4) for dx in range(4) for dc in range(2) if dy or dx or dc),
    key=lambda d: -min(d[0], 4 - d[0]) - min(d[1], 4 - d[1]),
)
CELLS = 32 * 128 * 128
NT = (((1,), (1,)), ((), ()))


def spot(y, x, core, z):
    return (
        (y * 2 + lax.div(x, 2)) * 2 + core,
        lax.rem(x, 2) * DEPTH + z,
    )


def body(
    source, preact, cotangent, kernel, gs_out, gk_out,
    pv, cv, sv, kv, wide, wide_src, wide_out, slope, src3, weights, prod_lo, prod_hi,
    part, half, plane_in, last, z_out, z_in,
    load_sem, halo_send, halo_recv, plane_send, plane_recv, z_send, z_recv,
):
    gx, gy = lax.axis_index("gx"), lax.axis_index("gy")
    core, xhi, y = lax.rem(gx, 2), lax.rem(lax.div(gx, 2), 2), lax.div(gx, 4)
    xlo, z = lax.div(gy, DEPTH), lax.rem(gy, DEPTH)
    x = xhi * 2 + xlo
    other = 1 - core

    up_x, dn_x = lax.rem(gx + 1, 16), lax.rem(gx + 15, 16)
    up_y, dn_y = lax.rem(gy + 1, 16), lax.rem(gy + 15, 16)

    loads = [
        pltpu.make_async_copy(src, dst, load_sem.at[n])
        for n, (src, dst) in enumerate(((preact, pv), (cotangent, cv), (source, sv), (kernel, kv)))
    ]
    for copy in loads:
        copy.start()

    plane_at, plane_to, z_to = [], [], []
    for dy, dx, dc in PLANE:
        to_core = other if dc else core
        to_y, to_x = lax.rem(y + dy, 4), lax.rem(x + dx, 4)
        plane_at.append(to_core * 16 + to_y * 4 + to_x)
        plane_to.append(spot(to_y, to_x, to_core, z))
    for k in range(1, DEPTH):
        z_to.append(spot(y, x, core, lax.rem(z + k, DEPTH)))
    sides = [
        (up_x, gy), (dn_x, gy), (gx, up_y), (gx, dn_y),
        (up_x, up_y), (up_x, dn_y), (dn_x, up_y), (dn_x, dn_y),
    ]
    everyone = sides + plane_to + z_to
    barrier = pltpu.get_barrier_semaphore()
    for device in everyone:
        pl.semaphore_signal(barrier, inc=1, device_id=device, device_id_type=MESH)

    loads[0].wait()
    loads[1].wait()
    for c in range(0, C, 8):
        keep = pv[c : c + 8].astype(F32) > 0
        masked = jnp.where(keep, cv[c : c + 8].astype(F32), 0.0)
        wide[c * 16 : c * 16 + 128, :] = masked.reshape(128, NZ)
    for i in range(WX):
        for j in range(WY):
            slope[i + 1, j + 1] = wide[pl.ds(i * WY + j, C, stride=WX * WY), :].astype(BF16)

    pl.semaphore_wait(barrier, len(everyone))
    ends = [
        (slope.at[2, 1:9], slope.at[0, 1:9]),
        (slope.at[1, 1:9], slope.at[3, 1:9]),
        (slope.at[1:3, 8], slope.at[1:3, 0]),
        (slope.at[1:3, 1], slope.at[1:3, 9]),
        (slope.at[2, 8], slope.at[0, 0]),
        (slope.at[2, 1], slope.at[0, 9]),
        (slope.at[1, 8], slope.at[3, 0]),
        (slope.at[1, 1], slope.at[3, 9]),
    ]
    halos = []
    for n, ((src, dst), device) in enumerate(zip(ends, sides)):
        copy = pltpu.make_async_remote_copy(
            src, dst, halo_send.at[n], halo_recv.at[n], device_id=device, device_id_type=MESH
        )
        copy.start()
        halos.append(copy)

    loads[2].wait()
    for c in range(0, C, 8):
        wide_src[c * 16 : c * 16 + 128, :] = sv[c : c + 8].astype(F32).reshape(128, NZ)
    for i in range(WX):
        for j in range(WY):
            block = wide_src[pl.ds(i * WY + j, C, stride=WX * WY), :]
            for c, shift in enumerate((1, 0, NZ - 1)):
                moved = pltpu.roll(block, shift, 1) if shift else block
                src3[i, j // 2, c * C : (c + 1) * C, (j % 2) * NZ : (j % 2 + 1) * NZ] = moved.astype(BF16)
    loads[3].wait()
    for c in range(3):
        for ab in range(0, 9, 2):
            taps = [kv[3 * n + c].astype(F32) for n in range(ab, min(ab + 2, 9))]
            pair = jnp.concatenate(taps, axis=0) if len(taps) > 1 else taps[0]
            weights[c * C : (c + 1) * C, ab * C : (ab + len(taps)) * C] = pair.T.astype(BF16)

    def columns(a, b, i, jp):
        return jnp.concatenate([slope[i + 2 - a, 2 * jp + 2 - b], slope[i + 2 - a, 2 * jp + 3 - b]], axis=1)

    for a in (1, 0, 2):
        for n in ((1, 6, 7), (2, 3), (0, 4, 5))[a]:
            halos[n].wait_recv()
        total = None
        for i in range(WX):
            for jp in range(WY // 2):
                left = jnp.concatenate([columns(a, b, i, jp) for b in range(3)], axis=0)
                term = lax.dot_general(left, src3[i, jp], NT, preferred_element_type=F32)
                total = term if total is None else total + term
        prod_lo[a * 192 : (a + 1) * 192, :] = total[:, :128]
        prod_hi[a * 192 : (a + 1) * 192, 0:C] = total[:, 128:]
        for b in range(3):
            base = (a * 3 + b) * C
            lo = [prod_lo[pl.ds(base + odd, 32, stride=2), :] for odd in (0, 1)]
            hi = [prod_hi[pl.ds(base + odd, 32, stride=2), :] for odd in (0, 1)]
            pairs = (
                jnp.concatenate([lo[0][:, :C], lo[1][:, :C]], axis=1),
                jnp.concatenate([lo[0][:, C:], lo[1][:, C:]], axis=1),
                jnp.concatenate([hi[0][:, :C], hi[1][:, :C]], axis=1),
            )
            for c, rows in enumerate(pairs):
                start = 32 * ((a * 3 + b) * 3 + c)
                at = start
                while at < start + 32:
                    q, r = divmod(at, ROWS)
                    count = min(ROWS - r, start + 32 - at)
                    part[(q >> 1) & 1, q >> 3, ((q >> 2) & 1) * 2 + (q & 1), r : r + count, :] = (
                        rows[at - start : at - start + count, :]
                    )
                    at += count

    def data_gradient(i):
        for jp in range(WY // 2):
            right = jnp.concatenate([columns(a, b, i, jp) for a in range(3) for b in range(3)], axis=0)
            out = jnp.dot(weights[...], right, preferred_element_type=F32)
            for half_at in range(2):
                three = [
                    out[c * C : (c + 1) * C, half_at * NZ : (half_at + 1) * NZ] for c in range(3)
                ]
                whole = pltpu.roll(three[0], NZ - 1, 1) + three[1] + pltpu.roll(three[2], 1, 1)
                wide_out[pl.ds(i * WY + 2 * jp + half_at, C, stride=WX * WY), :] = whole

    for c in range(2):
        for n in range(4):
            for m in range(4):
                half[c * 16 + n * 4 + m] = part[c, n, m].astype(BF16)
    plane_copies = []
    for k, (at, device) in enumerate(zip(plane_at, plane_to)):
        copy = pltpu.make_async_remote_copy(
            half.at[at], plane_in.at[k], plane_send.at[k], plane_recv.at[k],
            device_id=device, device_id_type=MESH,
        )
        copy.start()
        plane_copies.append(copy)

    data_gradient(0)
    data_gradient(1)
    for c in range(0, C, 8):
        gs_out[c : c + 8] = wide_out[c * 16 : c * 16 + 128, :].reshape(8, WX, WY, NZ).astype(BF16)

    total = part[core, y, x]
    for k in reversed(range(len(PLANE))):
        plane_copies[k].wait_recv()
        total = total + plane_in[k].astype(F32)
    last[...] = total
    lane = lax.broadcasted_iota(jnp.int32, (8, NZ), 1)
    for n in range(DEPTH):
        row, off = divmod(n * OWN, NZ)
        lower = last[row : row + 8, :]
        upper = last[row + 1 : row + 9, :]
        if off:
            lower = jnp.where(lane < NZ - off, pltpu.roll(lower, NZ - off, 1), pltpu.roll(upper, NZ - off, 1))
        z_out[n] = lower
    z_copies = []
    for k in range(1, DEPTH):
        copy = pltpu.make_async_remote_copy(
            z_out.at[lax.rem(z + k, DEPTH)], z_in.at[k - 1], z_send.at[k - 1], z_recv.at[k - 1],
            device_id=z_to[k - 1], device_id_type=MESH,
        )
        copy.start()
        z_copies.append(copy)
    for copy in z_copies:
        copy.wait_recv()
    mine = z_out[z]
    for k in range(DEPTH - 1):
        mine = mine + z_in[k]
    mine = mine * (1.0 / math.sqrt(CELLS))
    for row in range(0, OWN, NZ):
        count = min(NZ, OWN - row)
        gk_out[row : row + count] = mine[row // NZ, :count]

    for copy in halos + plane_copies + z_copies:
        copy.wait_send()


def on_device(source, preact, cotangent, kernel):
    dma = pltpu.SemaphoreType.DMA
    blocks = (WX + 2, WY + 2, C, NZ)
    grad_source, grad_kernel = pl.pallas_call(
        body,
        out_shape=(
            pltpu.VMEM(source.shape, BF16),
            pltpu.VMEM((OWN,), F32),
        ),
        in_specs=[pl.BlockSpec(memory_space=pl.ANY)] * 4,
        out_specs=(pl.BlockSpec(memory_space=pltpu.VMEM), pl.BlockSpec(memory_space=pltpu.VMEM)),
        scratch_shapes=[
            pltpu.VMEM(source.shape, BF16),
            pltpu.VMEM(source.shape, BF16),
            pltpu.VMEM(source.shape, BF16),
            pltpu.VMEM(kernel.shape, BF16),
            pltpu.VMEM((C * WX * WY, NZ), F32),
            pltpu.VMEM((C * WX * WY, NZ), F32),
            pltpu.VMEM((C * WX * WY, NZ), F32),
            pltpu.VMEM(blocks, BF16),
            pltpu.VMEM((WX, WY // 2, 3 * C, 2 * NZ), BF16),
            pltpu.VMEM((3 * C, 9 * C), BF16),
            pltpu.VMEM((9 * C, NZ), F32),
            pltpu.VMEM((9 * C, NZ), F32),
            pltpu.VMEM((2, 4, 4, 32, NZ), F32),
            pltpu.VMEM((32, 32, NZ), BF16),
            pltpu.VMEM((31, 32, NZ), BF16),
            pltpu.VMEM((32, NZ), F32),
            pltpu.VMEM((8, 8, NZ), F32),
            pltpu.VMEM((7, 8, NZ), F32),
            dma((4,)),
            dma((8,)), dma((8,)), dma((31,)), dma((31,)),
            dma((7,)), dma((7,)),
        ],
        compiler_params=pltpu.CompilerParams(collective_id=0, has_side_effects=True),
    )(source, preact, cotangent, kernel)
    return grad_source, grad_kernel


def solution(mesh):
    placed = (P(None, "gx", "gy", None), P(None, "gx", "gy", None), P(None, "gx", "gy", None), P())
    return jax.shard_map(
        on_device,
        mesh=mesh,
        in_specs=placed,
        out_specs=(P(None, "gx", "gy", None), P(("gx", "gy"))),
        check_vma=False,
    )
```
